32 devices in a mesh: dp: 8 (over z, x), seq: 4 (over y, core).
Axes of the slice: x: 2, y: 2, z: 4, core: 2. Of those that a mesh axis runs over, the one named last changes fastest.
Arguments:
- layer_input: bfloat16 [16, 1024, 512], P('dp', 'seq'), may hold values from -6 to 6
- memory: bfloat16 [16, 1024, 512], P('dp', 'seq'), may hold values from -6 to 6
- timesteps: int32 [16], P('dp'), may hold values from 0 to 49
- upstream: bfloat16 [16, 1024, 512], P('dp', 'seq'), may hold values from -6 to 6
- step_table: bfloat16 [50, 512], replicated, may hold values from -3 to 3
- norm_gains: float32 [3, 512], replicated, may hold values from 0.5 to 1.5
- shift_rows: float32 [10, 512], replicated, may hold values from -1.8 to 1.8
- self_entry: bfloat16 [512, 1536], replicated, may hold values from -0.25 to 0.25
- self_exit: bfloat16 [512, 512], replicated, may hold values from -4 to 4
- cross_query: bfloat16 [512, 512], replicated, may hold values from -0.25 to 0.25
- cross_keyval: bfloat16 [512, 1024], replicated, may hold values from -0.25 to 0.25
- cross_exit: bfloat16 [512, 512], replicated, may hold values from -4 to 4
- expand_weight: bfloat16 [512, 2048], replicated, may hold values from -0.25 to 0.25
- expand_bias: float32 [2048], replicated, may hold values from -1.8 to 1.8
- reduce_weight: bfloat16 [2048, 512], replicated, may hold values from -0.125 to 0.125
Outputs:
- result: float32 [16, 1024, 512], P('dp', 'seq')
- input_gradient: float32 [16, 1024, 512], P('dp', 'seq')
- memory_gradient: float32 [16, 1024, 512], P('dp', 'seq')
- table_gradient: float32 [50, 512], replicated
- gains_gradient: float32 [3, 512], replicated
- shifts_gradient: float32 [10, 512], replicated
- entry_gradient: float32 [512, 1536], replicated
- self_exit_gradient: float32 [512, 512], replicated
- cross_query_gradient: float32 [512, 512], replicated
- cross_keyval_gradient: float32 [512, 1024], replicated
- cross_exit_gradient: float32 [512, 512], replicated
- expand_gradient: float32 [512, 2048], replicated
- expand_bias_gradient: float32 [2048], replicated
- reduce_gradient: float32 [2048, 512], replicated
The draws below stay inside these ranges and needn't reach their ends.
All inputs are finite; a program needn't handle non-finite values.
Results may differ from the reference program's by a relative error of at most 0.017.
Values may be sent and summed in bfloat16 or wider, within the bound.
No kernel may reach another device: no remote copies, remote signals or barrier semaphores. Data moves between devices by JAX's collectives and lax.ppermute only.
A program may use at most 192 MiB of HBM per device.

```python
import math
import jax
import jax.numpy as jnp
from jax import lax

D = 512
H = 8
HD = 64
FF = 2048
STEPS = 50
SEG_LEN = 1024
SEGS = 16


def touch_ends(values, own_key, least, largest):
    shape = values.shape
    index_at = [jax.random.randint(jax.random.fold_in(own_key, axis), (), 0, shape[axis]) for axis in range(len(shape))]
    values = values.at[tuple(index_at)].set(least)
    longest = shape.index(max(shape))
    index_at[longest] = (index_at[longest] + 1) % shape[longest]
    return values.at[tuple(index_at)].set(largest)


def levels(key, extent, shards, low, largest):
    gain = 1.0
    for position, parts in shards:
        heights = jax.random.uniform(jax.random.fold_in(jax.random.fold_in(key, 6), position), (parts,), jnp.float32, low / len(shards), largest / len(shards))
        gain = gain * jnp.repeat(jnp.exp(heights), extent[position] // parts).reshape((-1,) + (1,) * (len(extent) - 1 - position))
    return gain


def centred(key, shape, width, most, cuts=(), dtype=jnp.bfloat16):
    drawn = width * jax.random.normal(key, shape, jnp.float32)
    if cuts:
        drawn = drawn * levels(key, shape, cuts, -0.22, 0.18)
    return jnp.clip(drawn, -most, most).astype(dtype)


def setup_inputs(seed: int = 0) -> dict:
    streams_of = jax.random.split(jax.random.key(seed), 16)
    return {
        "layer_input": centred(streams_of[0], (SEGS, SEG_LEN, D), 1.0, 6.0, ((0, 8), (1, 4))),
        "memory": centred(streams_of[1], (SEGS, SEG_LEN, D), 1.0, 6.0, ((0, 8), (1, 4))),
        "timesteps": touch_ends(jax.random.randint(streams_of[2], (SEGS,), 0, STEPS), jax.random.fold_in(streams_of[2], 1), 0, STEPS - 1).astype(jnp.int32),
        "upstream": centred(streams_of[3], (SEGS, SEG_LEN, D), 1.0, 6.0, ((0, 8), (1, 4))),
        "step_table": centred(streams_of[4], (STEPS, D), 0.5, 3.0),
        "norm_gains": jnp.clip(1.0 + 0.1 * jax.random.normal(streams_of[5], (3, D), jnp.float32), 0.5, 1.5),
        "shift_rows": centred(streams_of[6], (10, D), 0.3, 1.8, (), jnp.float32),
        "self_entry": centred(streams_of[7], (D, 3 * D), D ** -0.5, 0.25),
        "self_exit": centred(streams_of[8], (D, D), (max(1, D * 4 // SEG_LEN)) ** -0.5, 4.0),
        "cross_query": centred(streams_of[9], (D, D), D ** -0.5, 0.25),
        "cross_keyval": centred(streams_of[10], (D, 2 * D), D ** -0.5, 0.25),
        "cross_exit": centred(streams_of[11], (D, D), (max(1, D * 4 // SEG_LEN)) ** -0.5, 4.0),
        "expand_weight": centred(streams_of[12], (D, FF), D ** -0.5, 0.25),
        "expand_bias": centred(streams_of[13], (FF,), 0.3, 1.8, (), jnp.float32),
        "reduce_weight": centred(streams_of[14], (FF, D), FF ** -0.5, 0.125),
    }


EPSILON = 1e-05
EXACT = lax.Precision.HIGHEST

@jax.custom_vjp
def low(v):
    return lax.optimization_barrier(v.astype(jnp.bfloat16)).astype(jnp.float32)

@jax.custom_vjp
def low_back(v):
    return v

def low_keep(v):
    return (low(v), None)

def low_pass(kept, grad):
    return (grad,)

def back_keep(v):
    return (v, None)

def back_low(kept, grad):
    return (low(grad),)
low.defvjp(low_keep, low_pass)
low_back.defvjp(back_keep, back_low)

def both_ways(values):
    return low(low_back(values))

def layer_norm(values, norm_gain, norm_shift):
    centered = values - lax.optimization_barrier(jnp.mean(values, axis=-1, keepdims=True))
    inverse = lax.rsqrt(lax.optimization_barrier(jnp.mean(centered * centered, axis=-1, keepdims=True)) + EPSILON)
    return centered * inverse * norm_gain + norm_shift

def exact_dot(left, right):
    return jnp.dot(left, right, precision=EXACT)

def attention(queries, keys, values):
    split_queries = queries.reshape(queries.shape[0], H, HD)
    split_keys = keys.reshape(keys.shape[0], H, HD)
    split_values = values.reshape(values.shape[0], H, HD)
    scores = jnp.einsum('qhd,khd->hqk', split_queries, split_keys, precision=EXACT) * (1.0 / math.sqrt(HD))
    scores = low_back(scores)
    probability = low(jax.nn.softmax(scores, axis=-1))
    context = jnp.einsum('hqk,khd->qhd', probability, split_values, precision=EXACT)
    return context.reshape(queries.shape[0], D)

def segment_layer(parameters, segment_rows, memory_rows, timestep):
    step_table, norm_gains, shift_rows, self_entry, self_exit, cross_query, cross_keyval, cross_exit, expand_weight, expand_bias, reduce_weight = parameters
    hidden_one = layer_norm(segment_rows, norm_gains[0], shift_rows[0]) + step_table[timestep]
    normed_one = low(hidden_one)
    entry = exact_dot(normed_one, self_entry)
    queries = both_ways(entry[:, :D] + shift_rows[3])
    keys = both_ways(entry[:, D:2 * D])
    values = both_ways(entry[:, 2 * D:] + shift_rows[4])
    context_one = both_ways(attention(queries, keys, values))
    mixed_one = segment_rows + low_back(exact_dot(context_one, self_exit) + shift_rows[5])
    normed_two = low(layer_norm(mixed_one, norm_gains[1], shift_rows[1]))
    cross_queries = both_ways(exact_dot(normed_two, cross_query) + shift_rows[6])
    memory_proj = exact_dot(memory_rows, cross_keyval)
    memory_keys = both_ways(memory_proj[:, :D])
    memory_values = both_ways(memory_proj[:, D:] + shift_rows[7])
    context_two = both_ways(attention(cross_queries, memory_keys, memory_values))
    mixed_two = mixed_one + low_back(exact_dot(context_two, cross_exit) + shift_rows[8])
    normed_three = low(layer_norm(mixed_two, norm_gains[2], shift_rows[2]))
    expanded = low_back(exact_dot(normed_three, expand_weight) + expand_bias)
    activated = low(jax.nn.gelu(expanded, approximate=True))
    return mixed_two + exact_dot(activated, reduce_weight) + shift_rows[9]

def reference(layer_input, memory, timesteps, upstream, step_table, norm_gains, shift_rows, self_entry, self_exit, cross_query, cross_keyval, cross_exit, expand_weight, expand_bias, reduce_weight):
    parameters = tuple((weight.astype(jnp.float32) for weight in (step_table, norm_gains, shift_rows, self_entry, self_exit, cross_query, cross_keyval, cross_exit, expand_weight, expand_bias, reduce_weight)))
    inputs = layer_input.astype(jnp.float32)
    memory_rows = memory.astype(jnp.float32)
    layer_once = jax.checkpoint(segment_layer)

    def forward(parameters, inputs, memory_rows):
        return lax.map(lambda pieces: layer_once(parameters, pieces[0], pieces[1], pieces[2]), (inputs, memory_rows, timesteps))
    result, pullback = jax.vjp(forward, parameters, inputs, memory_rows)
    param_grads, input_gradient, memory_gradient = pullback(upstream.astype(jnp.float32))
    return (result, input_gradient, memory_gradient, param_grads[0], param_grads[1], param_grads[2], param_grads[3], param_grads[4], param_grads[5], param_grads[6], param_grads[7], param_grads[8], param_grads[9], param_grads[10])
```

```python
import functools
import math

import jax
import jax.numpy as jnp
from jax import lax
from jax.experimental import pallas as pl
from jax.experimental.pallas import tpu as pltpu
from jax.sharding import PartitionSpec as P

HD = 64
PAIR = 2 * HD
EPSILON = 1e-05
SCALING = 1.0 / math.sqrt(HD)
BF = jnp.bfloat16
F32 = jnp.float32
NT = (((1,), (1,)), ((), ()))
NN = (((1,), (0,)), ((), ()))
TN = (((0,), (0,)), ((), ()))


def dot(left, right, dims=NN):
    return lax.dot_general(left, right, dims, preferred_element_type=F32)


def norm_parts(values):
    centered = values - jnp.mean(values, axis=-1, keepdims=True)
    inverse = lax.rsqrt(jnp.mean(centered * centered, axis=-1, keepdims=True) + EPSILON)
    return centered * inverse, inverse


def norm_back(values, gain, incoming):
    unit, inverse = norm_parts(values)
    scaled = incoming * gain
    grad = inverse * (
        scaled
        - jnp.mean(scaled, axis=-1, keepdims=True)
        - unit * jnp.mean(scaled * unit, axis=-1, keepdims=True)
    )
    return grad, jnp.sum(incoming * unit, axis=0), jnp.sum(incoming, axis=0)


def column_sums(rows):
    return jnp.sum(rows.astype(F32), axis=0)


def attend_body(q_ref, k_ref, v_ref, o_ref, l_ref):
    lane = lax.broadcasted_iota(jnp.int32, (1, PAIR), 1)
    sub = lax.broadcasted_iota(jnp.int32, (PAIR, 1), 0)
    keys = k_ref[...]
    values = v_ref[...].T
    values = jnp.concatenate([values, jnp.ones((16, values.shape[1]), BF)], axis=0)
    queries = q_ref[...]
    outs = []
    for head in range(2):
        mine = (lane < HD) if head == 0 else (lane >= HD)
        scores = dot(keys, jnp.where(mine, queries, jnp.zeros_like(queries)), NT)
        top = jnp.max(scores, axis=0, keepdims=True)
        weight = jnp.exp(scores - top).astype(BF)
        summed = dot(values, weight)
        total = summed[PAIR : PAIR + 1]
        outs.append(summed[:PAIR] / total)
        l_ref[0, head : head + 1, :] = top + jnp.log(total)
    o_ref[...] = jnp.where(sub < HD, outs[0], outs[1]).T.astype(BF)


def attend(queries, keys, values):
    nq, width = queries.shape
    nk = keys.shape[0]
    pairs = width // PAIR
    row = lambda n: pl.BlockSpec((n, PAIR), lambda j: (0, j))
    return pl.pallas_call(
        attend_body,
        grid=(pairs,),
        in_specs=[row(nq), row(nk), row(nk)],
        out_specs=[row(nq), pl.BlockSpec((1, 2, nq), lambda j: (j, 0, 0))],
        out_shape=[
            jax.ShapeDtypeStruct((nq, width), BF),
            jax.ShapeDtypeStruct((pairs, 2, nq), F32),
        ],
        cost_estimate=pl.CostEstimate(
            flops=16 * nq * nk * width, bytes_accessed=4 * (nq + nk) * width, transcendentals=0
        ),
        name="attend",
    )(queries, keys, values)


def attend_back_body(tile, q_ref, k_ref, v_ref, o_ref, c_ref, l_ref, dq_ref, dk_ref, dv_ref):
    lane = lax.broadcasted_iota(jnp.int32, (1, PAIR), 1)
    sub = lax.broadcasted_iota(jnp.int32, (PAIR, 1), 0)
    queries = q_ref[...]
    incoming = c_ref[...]
    product = (incoming.astype(F32) * o_ref[...].astype(F32)).T
    inner = [
        jnp.sum(product[:HD], axis=0, keepdims=True),
        jnp.sum(product[HD:], axis=0, keepdims=True),
    ]
    one_q, one_c = [], []
    for head in range(2):
        mine = (lane < HD) if head == 0 else (lane >= HD)
        one_q.append(jnp.where(mine, queries, jnp.zeros_like(queries)))
        one_c.append(jnp.where(mine, incoming, jnp.zeros_like(incoming)))
    dq = [None, None]
    for start in range(0, k_ref.shape[0], tile):
        keys = k_ref[start : start + tile, :]
        values = v_ref[start : start + tile, :]
        turned = keys.T
        dk, dv = [], []
        for head in range(2):
            scores = dot(keys, one_q[head], NT)
            prob = jnp.exp(scores - l_ref[0, head : head + 1, :])
            prob_grad = dot(values, one_c[head], NT)
            score_grad = (prob * (prob_grad - inner[head])).astype(BF)
            dv.append(dot(prob.astype(BF), incoming))
            dk.append(dot(score_grad, queries))
            part = dot(turned, score_grad)
            dq[head] = part if dq[head] is None else dq[head] + part
        dk_ref[start : start + tile, :] = jnp.where(lane < HD, dk[0], dk[1]).astype(BF)
        dv_ref[start : start + tile, :] = jnp.where(lane < HD, dv[0], dv[1]).astype(BF)
    dq_ref[...] = (jnp.where(sub < HD, dq[0], dq[1]) * SCALING).T.astype(BF)


def attend_back(queries, keys, values, context, incoming, log_total):
    nq, width = queries.shape
    nk = keys.shape[0]
    pairs = width // PAIR
    row = lambda n: pl.BlockSpec((n, PAIR), lambda j: (0, j))
    return pl.pallas_call(
        functools.partial(attend_back_body, nk // 2),
        grid=(pairs,),
        in_specs=[
            row(nq),
            row(nk),
            row(nk),
            row(nq),
            row(nq),
            pl.BlockSpec((1, 2, nq), lambda j: (j, 0, 0)),
        ],
        out_specs=[row(nq), row(nk), row(nk)],
        out_shape=[
            jax.ShapeDtypeStruct((nq, width), BF),
            jax.ShapeDtypeStruct((nk, width), BF),
            jax.ShapeDtypeStruct((nk, width), BF),
        ],
        cost_estimate=pl.CostEstimate(
            flops=40 * nq * nk * width, bytes_accessed=6 * (nq + nk) * width, transcendentals=0
        ),
        name="attend_back",
    )(queries, keys, values, context, incoming, log_total)


def swap(value, axis, size, bit):
    return lax.ppermute(value, axis, [(i, i ^ (1 << bit)) for i in range(size)])


def rank_bit(axis, bit):
    return (lax.axis_index(axis) >> bit) & 1


def to_segments(value, chips):
    y = lax.axis_index("seq") // 2
    blocks = [lax.dynamic_index_in_dim(value, y, 0, keepdims=False)]
    for k in range(1, chips):
        out = lax.dynamic_index_in_dim(value, (y + k) % chips, 0, keepdims=False)
        pairs = [(i, (i + 2 * k) % (2 * chips)) for i in range(2 * chips)]
        blocks.append(lax.ppermute(out, "seq", pairs))
    return jnp.concatenate(blocks, axis=0)


def from_segments(value, chips, dtype=BF):
    y = lax.axis_index("seq") // 2
    rows = value.shape[0] // chips
    whole = jnp.zeros((chips, rows, value.shape[1]), F32)
    whole = lax.dynamic_update_index_in_dim(whole, value[:rows], y, 0)
    for k in range(1, chips):
        out = value[k * rows : (k + 1) * rows].astype(dtype)
        pairs = [(i, (i - 2 * k) % (2 * chips)) for i in range(2 * chips)]
        got = lax.ppermute(out, "seq", pairs).astype(F32)
        whole = lax.dynamic_update_index_in_dim(whole, got, (y + k) % chips, 0)
    return whole


def reduce_all(stack, bits, sizes):
    rows = stack.shape[1]
    levels = min(len(bits), int(math.log2(rows // 16)))
    value = stack
    for axis, bit in bits[:levels]:
        half = value.shape[1] // 2
        mine = rank_bit(axis, bit)
        away = lax.dynamic_slice_in_dim(value, (1 - mine) * half, half, 1)
        got = swap(away, axis, sizes[axis], bit)
        value = lax.dynamic_slice_in_dim(value, mine * half, half, 1)
        value = (value.astype(F32) + got.astype(F32)).astype(BF)
    for axis, bit in bits[levels:]:
        got = swap(value, axis, sizes[axis], bit)
        value = (value.astype(F32) + got.astype(F32)).astype(BF)
    for axis, bit in reversed(bits[:levels]):
        got = swap(value, axis, sizes[axis], bit)
        mine = rank_bit(axis, bit)
        value = jnp.where(
            mine == 0,
            jnp.concatenate([value, got], axis=1),
            jnp.concatenate([got, value], axis=1),
        )
    return value


def sum_all(value, bits, sizes):
    for axis, bit in bits:
        value = value + swap(value, axis, sizes[axis], bit)
    return value


def on_device(
    sizes,
    layer_input,
    memory,
    timesteps,
    upstream,
    step_table,
    norm_gains,
    shift_rows,
    self_entry,
    self_exit,
    cross_query,
    cross_keyval,
    cross_exit,
    expand_weight,
    expand_bias,
    reduce_weight,
):
    chips = sizes["seq"] // 2
    d = layer_input.shape[2]
    dp_bits = [("dp", b) for b in range(sizes["dp"].bit_length() - 1)]
    seq_bits = [("seq", b) for b in range(sizes["seq"].bit_length() - 1)]
    order_a = [seq_bits[0], dp_bits[0]] + seq_bits[1:] + dp_bits[1:]
    order_b = seq_bits + dp_bits

    x_own = to_segments(layer_input, chips)
    x_oth = swap(x_own, "seq", sizes["seq"], 0)
    m_own = to_segments(memory, chips)
    m_oth = swap(m_own, "seq", sizes["seq"], 0)
    up = to_segments(upstream, chips)
    step = lax.dynamic_index_in_dim(timesteps, lax.axis_index("seq") // 2, 0, keepdims=False)
    step_row = lax.dynamic_index_in_dim(step_table, step, 0).astype(F32)

    own = x_own.shape[0]
    x_all = jnp.concatenate([x_own, x_oth], axis=0)
    m_all = jnp.concatenate([m_own, m_oth], axis=0)
    inputs = x_all.astype(F32)
    unit, _ = norm_parts(inputs)
    normed_one = (unit * norm_gains[0] + shift_rows[0] + step_row).astype(BF)
    queries = (dot(normed_one[:own], self_entry[:, :d]) + shift_rows[3]).astype(BF) * BF(SCALING)
    keyval = dot(normed_one, self_entry[:, d:])
    keys = keyval[:, :d].astype(BF)
    values = (keyval[:, d:] + shift_rows[4]).astype(BF)
    context_one, log_one = attend(queries, keys, values)
    mixed_one = inputs[:own] + dot(context_one, self_exit) + shift_rows[5]
    unit, _ = norm_parts(mixed_one)
    normed_two = (unit * norm_gains[1] + shift_rows[1]).astype(BF)
    far_queries = (dot(normed_two, cross_query) + shift_rows[6]).astype(BF) * BF(SCALING)
    far = dot(m_all, cross_keyval)
    far_keys = far[:, :d].astype(BF)
    far_values = (far[:, d:] + shift_rows[7]).astype(BF)
    context_two, log_two = attend(far_queries, far_keys, far_values)
    mixed_two = mixed_one + dot(context_two, cross_exit) + shift_rows[8]
    unit, _ = norm_parts(mixed_two)
    normed_three = (unit * norm_gains[2] + shift_rows[2]).astype(BF)
    expanded = dot(normed_three, expand_weight) + expand_bias
    gelu = lambda u: jax.nn.gelu(u, approximate=True)
    activated, gelu_pull = jax.vjp(gelu, expanded)
    activated = activated.astype(BF)
    result = mixed_two + dot(activated, reduce_weight) + shift_rows[9]
    result = from_segments(result, chips)

    stacked = lambda left, right: jnp.stack(
        [dot(left, right[:, i : i + d], TN).astype(BF) for i in range(0, right.shape[1], d)]
    )
    reduce_grad = dot(activated, up, TN).astype(BF).reshape(-1, d, d)
    expanded_grad = gelu_pull(dot(up, reduce_weight, NT))[0].astype(BF)
    expand_grad = stacked(normed_three, expanded_grad)
    reduce_sum = reduce_all(reduce_grad, order_a, sizes)
    expand_sum = reduce_all(expand_grad, order_b, sizes)
    expand_bias_grad = column_sums(expanded_grad).reshape(-1, d)
    part, gain_three, shift_three = norm_back(
        mixed_two, norm_gains[2], dot(expanded_grad, expand_weight, NT)
    )
    mixed_two_grad = up.astype(F32) + part
    branch_two = mixed_two_grad.astype(BF)
    context_two_grad = dot(branch_two, cross_exit, NT).astype(BF)
    dq, dk, dv = attend_back(
        far_queries, far_keys, far_values, context_two, context_two_grad, log_two
    )
    cross_grads = jnp.stack(
        [
            dot(context_two, branch_two, TN).astype(BF),
            dot(normed_two, dq, TN).astype(BF),
            dot(m_all, dk, TN).astype(BF),
            dot(m_all, dv, TN).astype(BF),
        ]
    )
    cross_sum = reduce_all(cross_grads, order_a, sizes)
    far_query_shift = column_sums(dq)
    far_value_shift = column_sums(dv)
    memory_part = dot(dk, cross_keyval[:, :d], NT) + dot(dv, cross_keyval[:, d:], NT)
    got = swap(memory_part[own:].astype(BF), "seq", sizes["seq"], 0)
    memory_gradient = from_segments(memory_part[:own] + got.astype(F32), chips)

    part, gain_two, shift_two = norm_back(
        mixed_one, norm_gains[1], dot(dq, cross_query, NT)
    )
    mixed_one_grad = mixed_two_grad + part
    branch_one = mixed_one_grad.astype(BF)
    context_one_grad = dot(branch_one, self_exit, NT).astype(BF)
    dq, dk, dv = attend_back(queries, keys, values, context_one, context_one_grad, log_one)
    entry_grads = jnp.stack(
        [
            dot(context_one, branch_one, TN).astype(BF),
            dot(normed_one[:own], dq, TN).astype(BF),
            dot(normed_one, dk, TN).astype(BF),
            dot(normed_one, dv, TN).astype(BF),
        ]
    )
    entry_sum = reduce_all(entry_grads, order_b, sizes)
    hidden = dot(dk, self_entry[:, d : 2 * d], NT) + dot(dv, self_entry[:, 2 * d :], NT)
    hidden = hidden + jnp.concatenate(
        [dot(dq, self_entry[:, :d], NT), jnp.zeros((hidden.shape[0] - own, d), F32)]
    )
    part, gain_one, shift_one = norm_back(inputs, norm_gains[0], hidden)
    got = swap(part[own:].astype(BF), "seq", sizes["seq"], 0)
    input_gradient = from_segments(mixed_one_grad + part[:own] + got.astype(F32), chips)

    steps = step_table.shape[0]
    match = (jnp.arange(steps, dtype=jnp.int32) == step).astype(F32)
    table_grad = match[:, None] * jnp.sum(hidden, axis=0)[None, :]
    rows = [
        gain_one,
        gain_two,
        gain_three,
        shift_one,
        shift_two,
        shift_three,
        column_sums(dq),
        column_sums(dv),
        column_sums(branch_one),
        far_query_shift,
        far_value_shift,
        column_sums(branch_two),
        column_sums(up),
    ]
    small = jnp.concatenate([table_grad, jnp.stack(rows), expand_bias_grad], axis=0)
    small = sum_all(small, order_b, sizes)
    wide = lambda s: jnp.concatenate([s[i] for i in range(s.shape[0])], axis=1).astype(F32)
    return (
        result,
        input_gradient,
        memory_gradient,
        small[:steps],
        small[steps : steps + 3],
        small[steps + 3 : steps + 13],
        wide(entry_sum[1:]),
        entry_sum[0].astype(F32),
        cross_sum[1].astype(F32),
        wide(cross_sum[2:]),
        cross_sum[0].astype(F32),
        wide(expand_sum),
        small[steps + 13 :].reshape(-1),
        reduce_sum.reshape(-1, d).astype(F32),
    )


def solution(mesh):
    sizes = dict(mesh.shape)
    rows = P("dp", "seq", None)
    return jax.shard_map(
        functools.partial(on_device, sizes),
        mesh=mesh,
        in_specs=(rows, rows, P("dp"), rows) + (P(),) * 11,
        out_specs=(rows, rows, rows) + (P(),) * 11,
        check_vma=False,
    )
```
